32 devices in a mesh: fsdp: 8 (over z, x), tp: 4 (over y, core).
Axes of the slice: x: 2, y: 2, z: 4, core: 2. Of those that a mesh axis runs over, the one named last changes fastest.
Arguments:
- history: bfloat16 [8, 4096, 2048], P(None, 'fsdp'), may hold values from -6 to 6
- mix_in: float32 [4096, 32], P('fsdp'), may hold values from -2.4 to 2.4
- doc_positions: int32 [4096], P('fsdp'), may hold values from 0 to 2047, as said below
- gain_q: bfloat16 [2048], P('fsdp'), may hold values from 0.25 to 1.75
- gain_k: bfloat16 [2048], P('fsdp'), may hold values from 0.25 to 1.75
- gain_v: bfloat16 [2048], P('fsdp'), may hold values from 0.25 to 1.75
- gain_mlp: bfloat16 [2048], P('fsdp'), may hold values from 0.25 to 1.75
- gain_mix: bfloat16 [2048], P('fsdp'), may hold values from 0.25 to 1.75
- w_query: bfloat16 [2048, 2048], P('fsdp', 'tp'), may hold values from -0.125 to 0.125
- w_key: bfloat16 [2048, 2048], P('fsdp', 'tp'), may hold values from -0.125 to 0.125
- w_value: bfloat16 [2048, 2048], P('fsdp', 'tp'), may hold values from -0.125 to 0.125
- w_attn_out: bfloat16 [2048, 2048], P('fsdp', 'tp'), may hold values from -1 to 1
- w_mlp_in: bfloat16 [2048, 8192], P('fsdp', 'tp'), may hold values from -0.125 to 0.125
- w_mlp_out: bfloat16 [2048, 8192], P('fsdp', 'tp'), may hold values from -0.0625 to 0.0625
- w_mix_in: bfloat16 [2048, 36], P('fsdp'), may hold values from -0.125 to 0.125
- w_mix_out: bfloat16 [36, 36], replicated, may hold values from -1 to 1
- out_grad: bfloat16 [4096, 2048], P('fsdp'), may hold values from -6 to 6
- next_grad: float32 [4096, 36], P('fsdp'), may hold values from -6 to 6
Outputs:
- block_out: bfloat16 [4096, 2048], P('fsdp')
- next_mix: float32 [4096, 36], P('fsdp')
- history_grad: bfloat16 [8, 4096, 2048], P(None, 'fsdp')
- mix_grad: float32 [4096, 32], P('fsdp')
- grad_gain_q: float32 [2048], P('fsdp')
- grad_gain_k: float32 [2048], P('fsdp')
- grad_gain_v: float32 [2048], P('fsdp')
- grad_gain_mlp: float32 [2048], P('fsdp')
- grad_gain_mix: float32 [2048], P('fsdp')
- grad_w_query: float32 [2048, 2048], P('fsdp', 'tp')
- grad_w_key: float32 [2048, 2048], P('fsdp', 'tp')
- grad_w_value: float32 [2048, 2048], P('fsdp', 'tp')
- grad_w_attn_out: float32 [2048, 2048], P('fsdp', 'tp')
- grad_w_mlp_in: float32 [2048, 8192], P('fsdp', 'tp')
- grad_w_mlp_out: float32 [2048, 8192], P('fsdp', 'tp')
- grad_w_mix_in: float32 [2048, 36], P('fsdp')
- grad_w_mix_out: float32 [36, 36], replicated
The draws below stay inside these ranges and needn't reach their ends.
Inputs may be any that keep to these rules, and one draw needn't show every extreme that they name: `doc_positions`: documents are runs of consecutive tokens; every multiple of 2048 begins one, so no document crosses a sequence; the first sequence is a single document.
All inputs are finite; a program needn't handle non-finite values.
Results may differ from the reference program's by a relative error of at most 0.017.
Values may be sent and summed in bfloat16 or wider, within the bound.
A program may use at most 256 MiB of HBM per device.

```python
import math
import jax
import jax.numpy as jnp
from jax import lax

D = 2048
HEADS = 16
HD = 128
ROT = 32
FF = 8192
WAYS = 4
DEPTH = 8
MIXH = 36
SEQLEN = 2048
TOK_DEV = 512
TOKENS = 4096
NEXT = 36


def draw_doc_positions(key, part):
    token_index = jnp.arange(TOKENS, dtype=jnp.int32)
    starts = jax.random.randint(key, (TOKENS,), 0, TOK_DEV) == 0
    starts = starts & (token_index >= SEQLEN)
    starts = starts | (token_index % SEQLEN == 0)
    begin_index = lax.cummax(jnp.where(starts, token_index, 0), axis=0)
    return (token_index - begin_index).astype(jnp.int32)


def steps_of(stream_key, dims, cuts, low, largest):
    def one(position, shards_of):
        draws = jax.random.uniform(jax.random.fold_in(jax.random.fold_in(stream_key, 6), position), (shards_of,), jnp.float32, low / len(cuts), largest / len(cuts))
        return jnp.repeat(jnp.exp(draws), dims[position] // shards_of).reshape((-1,) + (1,) * (len(dims) - position - 1))

    gain = one(*cuts[0])
    for cut in cuts[1:]:
        gain = gain * one(*cut)
    return gain


def bell_draw(own_key, dims, spread, limit, shards=(), kind=jnp.bfloat16):
    result = jax.random.normal(own_key, dims, jnp.float32) * spread
    if len(shards) > 0:
        result = steps_of(own_key, dims, shards, -0.22, 0.18) * result
    return jnp.clip(result, min=-limit, max=limit).astype(kind)


def setup_inputs(seed: int = 0) -> dict:
    splits = jax.random.split(jax.random.key(seed), 19)
    history = bell_draw(splits[0], (DEPTH, TOKENS, D), 1.0, 6.0, ((1, 8),))
    mix_in = bell_draw(splits[1], (TOKENS, WAYS * DEPTH), 0.4, 2.4, ((0, 8),), jnp.float32)
    doc_positions = draw_doc_positions(jax.random.fold_in(splits[18], 71), 0)
    gain_q = jnp.clip(1.0 + 0.15 * jax.random.normal(splits[3], (D,), jnp.float32), 0.25, 1.75).astype(jnp.bfloat16)
    gain_k = jnp.clip(1.0 + 0.15 * jax.random.normal(splits[4], (D,), jnp.float32), 0.25, 1.75).astype(jnp.bfloat16)
    gain_v = jnp.clip(1.0 + 0.15 * jax.random.normal(splits[5], (D,), jnp.float32), 0.25, 1.75).astype(jnp.bfloat16)
    gain_mlp = jnp.clip(1.0 + 0.15 * jax.random.normal(splits[6], (D,), jnp.float32), 0.25, 1.75).astype(jnp.bfloat16)
    gain_mix = jnp.clip(1.0 + 0.15 * jax.random.normal(splits[7], (D,), jnp.float32), 0.25, 1.75).astype(jnp.bfloat16)
    w_query = bell_draw(splits[8], (D, D), D ** -0.5, 0.125, ((0, 8), (1, 4)))
    w_key = bell_draw(splits[9], (D, D), D ** -0.5, 0.125, ((0, 8), (1, 4)))
    w_value = bell_draw(splits[10], (D, D), D ** -0.5, 0.125, ((0, 8), (1, 4)))
    w_attn_out = bell_draw(splits[11], (D, D), (D // 64) ** -0.5, 1.0, ((0, 8), (1, 4)))
    w_mlp_in = bell_draw(splits[12], (D, FF), D ** -0.5, 0.125, ((0, 8), (1, 4)))
    w_mlp_out = bell_draw(splits[13], (D, FF), FF ** -0.5, 0.0625, ((0, 8), (1, 4)))
    w_mix_in = bell_draw(splits[14], (D, MIXH), D ** -0.5, 0.125, ((0, 8),))
    w_mix_out = bell_draw(splits[15], (MIXH, NEXT), MIXH ** -0.5, 1.0)
    out_grad = bell_draw(splits[16], (TOKENS, D), 1.0, 6.0, ((0, 8),))
    next_grad = bell_draw(splits[17], (TOKENS, NEXT), 1.0, 6.0, ((0, 8),), jnp.float32)
    return dict(history=history, mix_in=mix_in, doc_positions=doc_positions, gain_q=gain_q, gain_k=gain_k, gain_v=gain_v, gain_mlp=gain_mlp, gain_mix=gain_mix, w_query=w_query, w_key=w_key, w_value=w_value, w_attn_out=w_attn_out, w_mlp_in=w_mlp_in, w_mlp_out=w_mlp_out, w_mix_in=w_mix_in, w_mix_out=w_mix_out, out_grad=out_grad, next_grad=next_grad)


EPS = 1e-05
NEG = -1e+30

@jax.custom_vjp
def low(v):
    return lax.optimization_barrier(v.astype(jnp.bfloat16)).astype(jnp.float32)

@jax.custom_vjp
def low_back(v):
    return v

def low_keep(v):
    return (low(v), None)

def low_pass(kept, grad):
    return (grad,)

def back_keep(v):
    return (v, None)

def back_low(kept, grad):
    return (low(grad),)
low.defvjp(low_keep, low_pass)
low_back.defvjp(back_keep, back_low)

def layer_norm(values, gain_vec):
    centre = values - lax.optimization_barrier(jnp.mean(values, -1, keepdims=True))
    return centre * lax.rsqrt(lax.optimization_barrier(jnp.mean(centre * centre, -1, keepdims=True)) + EPS) * gain_vec

def rope_turn(values, positions, turn_sign):
    half_rot = ROT // 2
    frequency = 10000.0 ** (-2.0 * jnp.arange(half_rot, dtype=jnp.float32) / ROT)
    angle_table = positions.astype(jnp.float32)[:, None] * frequency[None, :]
    cosine = jnp.cos(angle_table)[:, None, :]
    sine_part = turn_sign * jnp.sin(angle_table)[:, None, :]
    lead_half = values[..., :half_rot]
    second = values[..., half_rot:ROT]
    return jnp.concatenate([lead_half * cosine - second * sine_part, second * cosine + lead_half * sine_part, values[..., ROT:]], -1)

def reference(history, mix_in, doc_positions, gain_q, gain_k, gain_v, gain_mlp, gain_mix, w_query, w_key, w_value, w_attn_out, w_mlp_in, w_mlp_out, w_mix_in, w_mix_out, out_grad, next_grad):
    highest = lax.Precision.HIGHEST
    head_scale = 1.0 / math.sqrt(HD)
    block_rows = min(512, SEQLEN)

    def matmul(left, right):
        return jnp.dot(left, right, precision=highest)

    def forward(hist_val, mix_val, gain_query, gain_keys, gain_values, gain_feed, gain_next, mat_query, mat_key, mat_value, mat_out, mat_up, mat_down, mat_first, mat_second):
        ways = jnp.einsum('tsj,jtd->std', mix_val.reshape(TOKENS, WAYS, DEPTH), hist_val, precision=highest)
        q_in = low(layer_norm(ways[0], gain_query))
        k_in = low(layer_norm(ways[1], gain_keys))
        v_in = low(layer_norm(ways[2], gain_values))
        queries = low(rope_turn(low_back(matmul(q_in, mat_query)).reshape(TOKENS, HEADS, HD), doc_positions, 1.0))
        key_rows = low(rope_turn(low_back(matmul(k_in, mat_key)).reshape(TOKENS, HEADS, HD), doc_positions, 1.0))
        value_rows = low(low_back(matmul(v_in, mat_value))).reshape(TOKENS, HEADS, HD)

        def attend_block(block_index):
            row_start = block_index.astype(jnp.int32) * block_rows
            seq_start = row_start // SEQLEN * SEQLEN
            query_block = lax.dynamic_slice_in_dim(queries, row_start, block_rows, 0)
            key_block = lax.dynamic_slice_in_dim(key_rows, seq_start, SEQLEN, 0)
            value_block = lax.dynamic_slice_in_dim(value_rows, seq_start, SEQLEN, 0)
            pos_block = lax.dynamic_slice_in_dim(doc_positions, row_start, block_rows, 0)
            query_index = row_start + jnp.arange(block_rows, dtype=jnp.int32)
            key_index = seq_start + jnp.arange(SEQLEN, dtype=jnp.int32)
            visible = (key_index[None, :] <= query_index[:, None]) & (key_index[None, :] >= (query_index - pos_block)[:, None])
            scores = low_back(jnp.einsum('qhd,khd->hqk', query_block, key_block, precision=highest) * head_scale)
            scores = jnp.where(visible[None], scores, NEG)
            row_top = lax.optimization_barrier(jnp.max(scores, -1, keepdims=True))
            expo = jnp.exp(scores - row_top)
            probabilities = expo / lax.optimization_barrier(jnp.sum(expo, -1, keepdims=True))
            return jnp.einsum('hqk,khd->qhd', low(probabilities), value_block, precision=highest)
        attended = lax.map(jax.checkpoint(attend_block), jnp.arange(TOKENS // block_rows, dtype=jnp.int32))
        attn_rows = low(low_back(attended.reshape(TOKENS, D)))
        residual = ways[3] + low_back(matmul(attn_rows, mat_out.T))
        mlp_in = low(layer_norm(residual, gain_feed))
        up_proj = low_back(matmul(mlp_in, mat_up))
        act_rows = low(jax.nn.gelu(up_proj, approximate=False))
        block_val = residual + low_back(matmul(act_rows, mat_down.T))
        next_val = matmul(jax.nn.gelu(matmul(layer_norm(block_val, gain_next), mat_first), approximate=False), mat_second)
        return (block_val, next_val)
    (block_val, next_val), pullback = jax.vjp(forward, history.astype(jnp.float32), mix_in, gain_q.astype(jnp.float32), gain_k.astype(jnp.float32), gain_v.astype(jnp.float32), gain_mlp.astype(jnp.float32), gain_mix.astype(jnp.float32), w_query.astype(jnp.float32), w_key.astype(jnp.float32), w_value.astype(jnp.float32), w_attn_out.astype(jnp.float32), w_mlp_in.astype(jnp.float32), w_mlp_out.astype(jnp.float32), w_mix_in.astype(jnp.float32), w_mix_out.astype(jnp.float32))
    gradients = pullback((out_grad.astype(jnp.float32), next_grad))
    return (block_val.astype(jnp.bfloat16), next_val, gradients[0].astype(jnp.bfloat16), gradients[1], gradients[2], gradients[3], gradients[4], gradients[5], gradients[6], gradients[7], gradients[8], gradients[9], gradients[10], gradients[11], gradients[12], gradients[13], gradients[14])
```

```python
import functools
import math

import jax
import jax.numpy as jnp
from jax import lax
from jax.experimental import pallas as pl
from jax.experimental.pallas import tpu as pltpu
from jax.sharding import PartitionSpec as P

HD = 128
ROT = 32
WAYS = 4
DEPTH = 8
SEQLEN = 2048
EPS = 1e-05
NEG = -1e30
F32 = jnp.float32
BF16 = jnp.bfloat16
VMEM_LIMIT = 56 * 2**20


def ring_order(count):
    return [2 * p if p < count // 2 else 2 * (count - 1 - p) + 1 for p in range(count)]


def ring_tables(count):
    order = ring_order(count)
    place = [0] * count
    for p, index in enumerate(order):
        place[index] = p
    return order, place


def ring_hop(value, order, base_count, by):
    size = len(order)
    pairs = []
    for start in range(0, base_count, size):
        pairs += [(start + order[p], start + order[(p + by) % size]) for p in range(size)]
    return lax.ppermute(value, "fsdp", pairs)


def swap_tp(value, bit):
    return lax.ppermute(value, "tp", [(i, i ^ bit) for i in range(lax.axis_size("tp"))])


def swap_fsdp(value, bit):
    return lax.ppermute(value, "fsdp", [(i, i ^ bit) for i in range(lax.axis_size("fsdp"))])


def after(value, *others):
    return lax.optimization_barrier((value, *others))[0]


class Ring:
    def __init__(self, size):
        self.total = lax.axis_size("fsdp")
        self.size = size
        if size == self.total:
            self.order, place = ring_tables(size)
        else:
            self.order, place = ring_tables(size)
        own = lax.axis_index("fsdp") % size
        self.own = own
        self.table = jnp.array(self.order, jnp.int32)
        self.place = jnp.array(place, jnp.int32)[own]

    def up(self, value):
        return ring_hop(value, self.order, self.total, 1)

    def down(self, value):
        return ring_hop(value, self.order, self.total, -1)

    def index(self, offset):
        return self.table[(self.place + offset) % self.size]


def ring_gather(ring, shard, start_after=()):
    rows = shard.shape[0]
    half = rows // 2
    if start_after:
        moving = after(shard, *start_after)
    else:
        moving = shard
    full = jnp.zeros((rows * ring.size,) + shard.shape[1:], shard.dtype)
    full = lax.dynamic_update_slice(full, shard, (ring.own * rows, 0))
    going_up, going_down = moving[:half], moving[half:]
    marks = []
    for step in range(1, ring.size):
        going_up, going_down = ring.up(going_up), ring.down(going_down)
        full = lax.dynamic_update_slice(full, going_up, (ring.index(-step) * rows, 0))
        full = lax.dynamic_update_slice(full, going_down, (ring.index(step) * rows + half, 0))
        marks.append((going_up, going_down))
    return full, marks


def ring_reduce(ring, rows, block):
    half = rows // 2
    going_up = going_down = None
    for step in range(1, ring.size + 1):
        up_block = block(ring.index(-step) * rows, half)
        down_block = block(ring.index(step) * rows + half, half)
        if step > 1:
            up_block = up_block + going_up.astype(F32)
            down_block = down_block + going_down.astype(F32)
        if step == ring.size:
            return jnp.concatenate([up_block, down_block], 0)
        going_up, going_down = ring.up(up_block.astype(BF16)), ring.down(down_block.astype(BF16))


def small_gather(value):
    own = lax.axis_index("fsdp")
    bit = 1
    while bit < lax.axis_size("fsdp"):
        other = swap_fsdp(value, bit)
        value = jnp.where(
            (own & bit) == 0,
            jnp.concatenate([value, other], 1),
            jnp.concatenate([other, value], 1),
        )
        bit *= 2
    return value


def small_scatter(value):
    own = lax.axis_index("fsdp")
    value = value + swap_tp(value, 1)
    value = value + swap_tp(value, 2)
    bit = lax.axis_size("fsdp") // 2
    while bit >= 1:
        width = value.shape[1] // 2
        low, high = value[:, :width], value[:, width:]
        is_low = (own & bit) == 0
        value = jnp.where(is_low, low, high) + swap_fsdp(jnp.where(is_low, high, low), bit)
        bit //= 2
    return value


def small_sum(value):
    value = value + swap_tp(value, 1)
    value = value + swap_tp(value, 2)
    bit = lax.axis_size("fsdp") // 2
    while bit >= 1:
        value = value + swap_fsdp(value, bit)
        bit //= 2
    return value


class Quarter:
    def __init__(self, tokens):
        tp_index = lax.axis_index("tp")
        self.core = tp_index % 2
        self.side = tp_index // 2
        self.half = tokens // 2
        self.rows = tokens // 4
        self.start = self.core * self.half + self.side * self.rows

    def own(self, value):
        return lax.dynamic_slice_in_dim(value, self.start, self.rows, 0)

    def total(self, product):
        away = product((1 - self.core) * self.half, self.half).astype(BF16)
        here = product(self.core * self.half, self.half)
        chip = here + swap_tp(away, 1).astype(F32)
        keep = lax.dynamic_slice_in_dim(chip, self.side * self.rows, self.rows, 0)
        send = lax.dynamic_slice_in_dim(chip, (1 - self.side) * self.rows, self.rows, 0)
        return keep + swap_tp(send.astype(BF16), 2).astype(F32)

    def gather(self, value):
        other = swap_tp(value, 2)
        half = jnp.where(
            self.side == 0,
            jnp.concatenate([value, other], 0),
            jnp.concatenate([other, value], 0),
        )
        far = swap_tp(half, 1)
        return jnp.where(
            self.core == 0,
            jnp.concatenate([half, far], 0),
            jnp.concatenate([far, half], 0),
        )


def gelu_exact(values):
    return jax.nn.gelu(values, approximate=False)


def normed(values):
    centre = values - jnp.mean(values, -1, keepdims=True)
    scale = lax.rsqrt(jnp.mean(centre * centre, -1, keepdims=True) + EPS)
    return centre * scale, scale


def norm_back(grad, gain_row, hat, scale):
    inner = grad * gain_row
    grad_values = scale * (
        inner
        - jnp.mean(inner, -1, keepdims=True)
        - hat * jnp.mean(inner * hat, -1, keepdims=True)
    )
    return grad_values, jnp.sum(grad * hat, 0)


def mix_ways(mix_rows, history_rows, way_list):
    ways = []
    for way in way_list:
        total = None
        for depth in range(DEPTH):
            column = way * DEPTH + depth
            term = mix_rows[:, column : column + 1] * history_rows[depth].astype(F32)
            total = term if total is None else total + term
        ways.append(total)
    return ways


def rope_tables(positions):
    half_rot = ROT // 2
    frequency = 10000.0 ** (-2.0 * jnp.arange(half_rot, dtype=F32) / ROT)
    angle = positions.astype(F32)[:, None] * frequency[None, :]
    cosine, sine = jnp.cos(angle), jnp.sin(angle)
    rest = HD - ROT
    count = positions.shape[0]
    straight = jnp.concatenate([cosine, cosine, jnp.ones((count, rest), F32)], 1)
    crossed = jnp.concatenate([-sine, sine, jnp.zeros((count, rest), F32)], 1)
    return straight, crossed


def rope_in_kernel(value, straight, crossed):
    half_rot = ROT // 2
    lane = lax.broadcasted_iota(jnp.int32, value.shape, 1)
    partner = jnp.where(
        lane < half_rot,
        pltpu.roll(value, HD - half_rot, 1),
        pltpu.roll(value, half_rot, 1),
    )
    return value * straight + partner * crossed


def project_kernel(q_in, k_in, v_in, wq, wk, wv, straight, crossed, q_out, k_out, v_out):
    even, odd = straight[...], crossed[...]
    heads = q_out.shape[1] // HD
    for source, weight, target in ((q_in, wq, q_out), (k_in, wk, k_out)):
        raw = jnp.dot(source[...], weight[...], preferred_element_type=F32)
        for head in range(heads):
            cut = slice(head * HD, (head + 1) * HD)
            target[:, cut] = rope_in_kernel(raw[:, cut], even, odd).astype(BF16)
    v_out[...] = jnp.dot(v_in[...], wv[...], preferred_element_type=F32).astype(BF16)


def project(q_in, k_in, v_in, wq, wk, wv, straight, crossed):
    tokens, width = q_in.shape
    columns = wq.shape[1]
    step = 2 * HD
    rows = pl.BlockSpec((tokens, width), lambda i: (0, 0))
    weight = pl.BlockSpec((width, step), lambda i: (0, i))
    table = pl.BlockSpec((tokens, HD), lambda i: (0, 0))
    out = pl.BlockSpec((tokens, step), lambda i: (0, i))
    shape = jax.ShapeDtypeStruct((tokens, columns), BF16)
    return pl.pallas_call(
        project_kernel,
        grid=(columns // step,),
        in_specs=[rows] * 3 + [weight] * 3 + [table] * 2,
        out_specs=[out] * 3,
        out_shape=[shape] * 3,
        compiler_params=pltpu.CompilerParams(vmem_limit_bytes=VMEM_LIMIT),
        cost_estimate=pl.CostEstimate(
            flops=6 * tokens * width * columns,
            bytes_accessed=6 * tokens * width + 6 * width * columns + 6 * tokens * columns,
            transcendentals=0,
        ),
        name="project",
    )(q_in, k_in, v_in, wq, wk, wv, straight, crossed)


def visible_mask(shape, query_start, first_seen):
    key_index = lax.broadcasted_iota(jnp.int32, shape, 1)
    query_index = query_start + lax.broadcasted_iota(jnp.int32, (shape[0], 1), 0)
    return (key_index <= query_index) & (key_index >= query_index - first_seen)


def attend_kernel(base, positions, q_ref, k_ref, v_ref, out_ref, low_ref, lse_ref):
    block = q_ref.shape[0]
    start = base[0] + pl.program_id(1) * block
    scores = lax.dot_general(
        q_ref[...], k_ref[...], (((1,), (1,)), ((), ())), preferred_element_type=F32
    ) * (1.0 / math.sqrt(HD))
    seen = visible_mask(scores.shape, start, positions[...])
    scores = jnp.where(seen, scores, NEG)
    top = jnp.max(scores, 1, keepdims=True)
    weights = jnp.exp(scores - top)
    total = jnp.sum(weights, 1, keepdims=True)
    mixed = jnp.dot(weights.astype(BF16), v_ref[...], preferred_element_type=F32) / total
    out_ref[...] = mixed
    low_ref[...] = mixed.astype(BF16)
    lse_ref[...] = jnp.broadcast_to(top + jnp.log(total), lse_ref.shape)


def attend(queries, keys, values, positions, base):
    tokens, columns = queries.shape
    heads = columns // HD
    length = keys.shape[0]
    block = min(128, tokens)
    q_spec = pl.BlockSpec((block, HD), lambda h, i: (i, h))
    kv_spec = pl.BlockSpec((length, HD), lambda h, i: (0, h))
    return pl.pallas_call(
        attend_kernel,
        grid=(heads, tokens // block),
        in_specs=[
            pl.BlockSpec(memory_space=pltpu.SMEM),
            pl.BlockSpec((block, 1), lambda h, i: (i, 0)),
            q_spec,
            kv_spec,
            kv_spec,
        ],
        out_specs=[q_spec, q_spec, q_spec],
        out_shape=[
            jax.ShapeDtypeStruct((tokens, columns), F32),
            jax.ShapeDtypeStruct((tokens, columns), BF16),
            jax.ShapeDtypeStruct((tokens, columns), F32),
        ],
        compiler_params=pltpu.CompilerParams(vmem_limit_bytes=VMEM_LIMIT),
        cost_estimate=pl.CostEstimate(
            flops=4 * tokens * length * columns,
            bytes_accessed=4 * length * columns + 12 * tokens * columns,
            transcendentals=tokens * length * heads,
        ),
        name="attend",
    )(base, positions, queries, keys, values)


def attend_back_kernel(
    base, positions, straight, crossed, q_ref, k_ref, v_ref, g_ref, out_ref, lse_ref,
    gq_ref, gk_ref, gv_ref,
):
    step = pl.program_id(1)
    block = q_ref.shape[0]
    scale = 1.0 / math.sqrt(HD)
    start = base[0] + step * block
    queries, keys, values, grad = q_ref[...], k_ref[...], v_ref[...], g_ref[...]
    across = (((1,), (1,)), ((), ()))
    down = (((0,), (0,)), ((), ()))
    delta = jnp.sum(grad.astype(F32) * out_ref[...], 1, keepdims=True)
    scores = lax.dot_general(queries, keys, across, preferred_element_type=F32) * scale
    seen = visible_mask(scores.shape, start, positions[...])
    probs = jnp.where(seen, jnp.exp(scores - lse_ref[:, :1]), 0.0)
    grad_probs = lax.dot_general(grad, values, across, preferred_element_type=F32)
    grad_scores = (probs * (grad_probs - delta)).astype(BF16)
    grad_query = jnp.dot(grad_scores, keys, preferred_element_type=F32) * scale
    gq_ref[...] = rope_in_kernel(grad_query, straight[...], -crossed[...]).astype(BF16)
    grad_key = lax.dot_general(grad_scores, queries, down, preferred_element_type=F32) * scale
    grad_value = lax.dot_general(probs.astype(BF16), grad, down, preferred_element_type=F32)

    @pl.when(step == 0)
    def _():
        gk_ref[...] = grad_key
        gv_ref[...] = grad_value

    @pl.when(step > 0)
    def _():
        gk_ref[...] += grad_key
        gv_ref[...] += grad_value


def attend_back(queries, keys, values, grad, out, lse, positions, base, straight, crossed):
    tokens, columns = queries.shape
    heads = columns // HD
    length = keys.shape[0]
    block = min(128, tokens)
    q_spec = pl.BlockSpec((block, HD), lambda h, i: (i, h))
    kv_spec = pl.BlockSpec((length, HD), lambda h, i: (0, h))
    table = pl.BlockSpec((block, HD), lambda h, i: (i, 0))
    return pl.pallas_call(
        attend_back_kernel,
        grid=(heads, tokens // block),
        in_specs=[
            pl.BlockSpec(memory_space=pltpu.SMEM),
            pl.BlockSpec((block, 1), lambda h, i: (i, 0)),
            table,
            table,
            q_spec,
            kv_spec,
            kv_spec,
            q_spec,
            q_spec,
            q_spec,
        ],
        out_specs=[q_spec, kv_spec, kv_spec],
        out_shape=[
            jax.ShapeDtypeStruct((tokens, columns), BF16),
            jax.ShapeDtypeStruct((length, columns), F32),
            jax.ShapeDtypeStruct((length, columns), F32),
        ],
        compiler_params=pltpu.CompilerParams(vmem_limit_bytes=VMEM_LIMIT),
        cost_estimate=pl.CostEstimate(
            flops=10 * tokens * length * columns,
            bytes_accessed=12 * length * columns + 14 * tokens * columns,
            transcendentals=tokens * length * heads,
        ),
        name="attend_back",
    )(base, positions, straight, crossed, queries, keys, values, grad, out, lse)


def turn_back_kernel(value_ref, straight, crossed, out_ref):
    for head in range(value_ref.shape[1] // HD):
        cut = slice(head * HD, (head + 1) * HD)
        out_ref[:, cut] = rope_in_kernel(
            value_ref[:, cut], straight[...], -crossed[...]
        ).astype(BF16)


def turn_back(value, straight, crossed):
    return pl.pallas_call(
        turn_back_kernel,
        out_shape=jax.ShapeDtypeStruct(value.shape, BF16),
        compiler_params=pltpu.CompilerParams(vmem_limit_bytes=VMEM_LIMIT),
        cost_estimate=pl.CostEstimate(
            flops=4 * value.size, bytes_accessed=6 * value.size, transcendentals=0
        ),
        name="turn_back",
    )(value, straight, crossed)


def dot_f32(left, right):
    return jnp.dot(left, right, preferred_element_type=F32)


def dot_cols(left, right):
    return lax.dot_general(left, right, (((1,), (1,)), ((), ())), preferred_element_type=F32)


def rows_of(left, right):
    def product(start, count):
        return dot_cols(lax.dynamic_slice_in_dim(left, start, count, 0), right)

    return product


def weight_block(left, right):
    def block(start, count):
        part = lax.dynamic_slice_in_dim(left, start, count, 1)
        return lax.dot_general(part, right, (((0,), (0,)), ((), ())), preferred_element_type=F32)

    return block


def local(
    history,
    mix_in,
    doc_positions,
    gain_q,
    gain_k,
    gain_v,
    gain_mlp,
    gain_mix,
    w_query,
    w_key,
    w_value,
    w_attn_out,
    w_mlp_in,
    w_mlp_out,
    w_mix_in,
    w_mix_out,
    out_grad,
    next_grad,
):
    tokens = history.shape[1]
    shard_rows, columns = w_query.shape
    group_size = SEQLEN // tokens
    highest = lax.Precision.HIGHEST
    ring = Ring(lax.axis_size("fsdp"))
    group = Ring(group_size)
    quarter = Quarter(tokens)

    small = jnp.concatenate(
        [jnp.stack([gain_q, gain_k, gain_v, gain_mlp, gain_mix], 0), w_mix_in.T], 0
    )
    small_all = small_gather(small).astype(F32)
    gain_rows = [small_all[i : i + 1] for i in range(5)]
    first_mix = small_all[5:]
    second_mix = w_mix_out.astype(F32)
    qk_all, qk_marks = ring_gather(ring, jnp.concatenate([w_query, w_key], 1))
    vo_all, vo_marks = ring_gather(ring, jnp.concatenate([w_value, w_attn_out], 1))
    hold = (*qk_marks[-2], *vo_marks[-2])
    wi_all, _ = ring_gather(ring, w_mlp_in, hold)
    wf_all, _ = ring_gather(ring, w_mlp_out, hold)
    wq_all, wk_all = qk_all[:, :columns], qk_all[:, columns:]
    wv_all, wo_all = vo_all[:, :columns], vo_all[:, columns:]

    ways = mix_ways(mix_in, history, range(3))
    ins = [
        (normed(way)[0] * gain_row).astype(BF16)
        for way, gain_row in zip(ways, gain_rows[:3], strict=True)
    ]
    q_in, k_in, v_in = ins
    straight, crossed = rope_tables(doc_positions)
    queries, keys, values = project(q_in, k_in, v_in, wq_all, wk_all, wv_all, straight, crossed)

    keys_all = jnp.zeros((tokens * group_size, columns), BF16)
    values_all = jnp.zeros((tokens * group_size, columns), BF16)
    keys_all = lax.dynamic_update_slice(keys_all, keys, (group.own * tokens, 0))
    values_all = lax.dynamic_update_slice(values_all, values, (group.own * tokens, 0))
    moving_keys, moving_values = keys, values
    for step in range(1, group_size):
        moving_keys, moving_values = group.up(moving_keys), group.down(moving_values)
        keys_all = lax.dynamic_update_slice(
            keys_all, moving_keys, (group.index(-step) * tokens, 0)
        )
        values_all = lax.dynamic_update_slice(
            values_all, moving_values, (group.index(step) * tokens, 0)
        )
    position_column = doc_positions[:, None]
    base = (group.own * tokens).astype(jnp.int32)[None]
    attn, attn_low, lse = attend(queries, keys_all, values_all, position_column, base)

    own_mix = quarter.own(mix_in)
    own_history = lax.dynamic_slice_in_dim(history, quarter.start, quarter.rows, 1)
    own_ways = mix_ways(own_mix, own_history, range(WAYS))
    residual = own_ways[3] + quarter.total(rows_of(attn_low, wo_all))
    res_hat, res_scale = normed(residual)
    mlp_in = quarter.gather((res_hat * gain_rows[3]).astype(BF16))

    up_proj = dot_f32(mlp_in, wi_all)
    act_rows = gelu_exact(up_proj).astype(BF16)
    block_val = residual + quarter.total(rows_of(act_rows, wf_all))

    block_hat, block_scale = normed(block_val)
    hidden_raw = lax.dot_general(
        block_hat * gain_rows[4], first_mix, (((1,), (1,)), ((), ())), precision=highest
    )
    hidden, gelu_pullback = jax.vjp(gelu_exact, hidden_raw)
    next_own = jnp.dot(hidden, second_mix, precision=highest)
    own_next_grad = quarter.own(next_grad)
    g_hidden = lax.dot_general(
        own_next_grad, second_mix, (((1,), (1,)), ((), ())), precision=highest
    )
    g_second = lax.dot_general(
        hidden, own_next_grad, (((0,), (0,)), ((), ())), precision=highest
    )
    g_hidden_raw = gelu_pullback(g_hidden)[0]
    g_mix_norm = jnp.dot(g_hidden_raw, first_mix, precision=highest)
    g_first = lax.dot_general(
        g_hidden_raw, block_hat * gain_rows[4], (((0,), (0,)), ((), ())), precision=highest
    )
    g_block_mix, g_gain_mix = norm_back(g_mix_norm, gain_rows[4], block_hat, block_scale)
    g_block = quarter.own(out_grad).astype(F32) + g_block_mix
    g_block_low = quarter.gather(g_block.astype(BF16))

    g_act = dot_f32(g_block_low, wf_all)
    g_up = jax.vjp(gelu_exact, up_proj)[1](g_act)[0].astype(BF16)
    g_mlp_in = quarter.total(rows_of(g_up, wi_all))
    grad_mlp_out = ring_reduce(ring, shard_rows, weight_block(g_block_low, act_rows))
    grad_mlp_in = ring_reduce(ring, shard_rows, weight_block(mlp_in, g_up))
    g_res_norm, g_gain_mlp = norm_back(g_mlp_in, gain_rows[3], res_hat, res_scale)
    g_res = g_block + g_res_norm
    g_res_low = quarter.gather(g_res.astype(BF16))

    g_attn = dot_f32(g_res_low, wo_all).astype(BF16)
    g_q_raw, g_keys_part, g_values_part = attend_back(
        queries, keys_all, values_all, g_attn, attn, lse, position_column, base, straight, crossed
    )
    moving_keys = moving_values = None
    for step in range(1, group_size + 1):
        key_block = lax.dynamic_slice_in_dim(
            g_keys_part, group.index(-step) * tokens, tokens, 0
        )
        value_block = lax.dynamic_slice_in_dim(
            g_values_part, group.index(step) * tokens, tokens, 0
        )
        if step > 1:
            key_block = key_block + moving_keys.astype(F32)
            value_block = value_block + moving_values.astype(F32)
        if step < group_size:
            moving_keys = group.up(key_block.astype(BF16))
            moving_values = group.down(value_block.astype(BF16))
    g_k_raw = turn_back(key_block, straight, crossed)
    g_v_raw = value_block.astype(BF16)

    grad_attn_out = ring_reduce(ring, shard_rows, weight_block(g_res_low, attn_low))
    grad_query = ring_reduce(ring, shard_rows, weight_block(q_in, g_q_raw))
    grad_key = ring_reduce(ring, shard_rows, weight_block(k_in, g_k_raw))
    grad_value = ring_reduce(ring, shard_rows, weight_block(v_in, g_v_raw))

    way_grads_own, way_gains, way_grads = [], [], []
    for index, (raw, weight) in enumerate(
        ((g_q_raw, wq_all), (g_k_raw, wk_all), (g_v_raw, wv_all))
    ):
        grad_in = quarter.total(rows_of(raw, weight))
        hat, scale = normed(own_ways[index])
        grad_way, grad_gain = norm_back(grad_in, gain_rows[index], hat, scale)
        way_grads_own.append(grad_way)
        way_gains.append(grad_gain)
        way_grads.append(quarter.gather(grad_way.astype(BF16)).astype(F32))
    way_grads_own.append(g_res)
    way_grads.append(g_res_low.astype(F32))
    history_parts = []
    for depth in range(DEPTH):
        total = None
        for way in range(WAYS):
            column = way * DEPTH + depth
            term = mix_in[:, column : column + 1] * way_grads[way]
            total = term if total is None else total + term
        history_parts.append(total.astype(BF16))
    history_grad = jnp.stack(history_parts, 0)
    mix_columns = []
    for way in range(WAYS):
        for depth in range(DEPTH):
            mix_columns.append(jnp.sum(way_grads_own[way] * own_history[depth].astype(F32), -1))
    mix_grad = quarter.gather(jnp.stack(mix_columns, 1))

    early = small_scatter(jnp.concatenate([jnp.stack([g_gain_mlp, g_gain_mix], 0), g_first], 0))
    late = small_scatter(jnp.stack(way_gains, 0))
    grad_mix_out = small_sum(g_second)
    block_out = quarter.gather(block_val.astype(BF16))
    next_mix = quarter.gather(next_own)
    return (
        block_out,
        next_mix,
        history_grad,
        mix_grad,
        late[0],
        late[1],
        late[2],
        early[0],
        early[1],
        grad_query,
        grad_key,
        grad_value,
        grad_attn_out,
        grad_mlp_in,
        grad_mlp_out,
        early[2:].T,
        grad_mix_out,
    )


def solution(mesh):
    rows, vector, weight = P("fsdp", None), P("fsdp"), P("fsdp", "tp")
    stored = P(None, "fsdp", None)
    in_specs = (
        (stored, rows) + (vector,) * 6 + (weight,) * 6 + (rows, P(), rows, rows)
    )
    out_specs = (rows, rows, stored, rows) + (vector,) * 5 + (weight,) * 6 + (rows, P())
    return jax.shard_map(local, mesh=mesh, in_specs=in_specs, out_specs=out_specs, check_vma=False)
```
